32 devices in a mesh: blocks: 2 (over y), stripe: 4 (over z), cond: 2 (over x), col: 2 (over core).
Axes of the slice: x: 2, y: 2, z: 4, core: 2. Of those that a mesh axis runs over, the one named last changes fastest.
Arguments:
- theta: float32 [1024, 512], P(('blocks', 'stripe', 'cond'), 'col'), parts along dimension 0, may hold values from -6 to 6
- seed_map: int32 [1024, 512], P(('blocks', 'stripe', 'cond'), 'col'), parts along dimension 0, may hold values 0 or 1
- target: bfloat16 [1024, 512], P(('blocks', 'stripe'), 'col'), parts along dimension 0, may hold values from 0 to 1
- row_taps: bfloat16 [5, 6, 129], replicated, may hold values from -0.5 to 0.5
- col_taps: bfloat16 [5, 6, 129], replicated, may hold values from -0.5 to 0.5
- kernel_weight: float32 [5, 6], replicated, may hold values from 0.05 to 0.4
- cond_index: int32 [4], P('cond'), may hold values from 0 to 4
- dose: float32 [4], P('cond'), may hold values from 0.7 to 1.4
Outputs:
- grad_theta: float32 [1024, 512], P(('blocks', 'stripe', 'cond'), 'col'), parts along dimension 0
The draws below stay inside these ranges and needn't reach their ends.
There are 2 independent parts, one for each index of `blocks`. The reference program is written for one: setup_inputs(seed, part) draws one part's arguments, and reference() takes and returns one part's arrays. A program takes and returns all parts, laid end to end along the dimension named above; an argument that names none is the same for every part. Nothing has to cross between parts.
All inputs are finite; a program needn't handle non-finite values. No bound on the sum of `seed_map` on one device may be relied on, other than what follows from the above.
Results may differ from the reference program's by a relative error of at most 0.0059.
Values may be sent and summed in bfloat16 or wider, within the bound.
A program may use at most 64 MiB of HBM per device.

```python
import math
import jax
import jax.numpy as jnp
from jax import lax

HALF = 64
TAPS = 129
KERNELS = 6
FOCUS = 5
CONDS = 4
NR = 512
NC = 512


def touch_ends(values, rng, least, top_value):
    shape = values.shape
    place = [jax.random.randint(jax.random.fold_in(rng, axis), (), 0, shape[axis]) for axis in range(len(shape))]
    values = values.at[tuple(place)].set(least)
    longest = shape.index(max(shape))
    place[longest] = (place[longest] + 1) % shape[longest]
    return values.at[tuple(place)].set(top_value)


def steps_of(own_key, dims, split, least, top_value):
    gain = 1.0
    for axis_at, parts in split:
        steps = jax.random.uniform(jax.random.fold_in(jax.random.fold_in(own_key, 6), axis_at), (parts,), jnp.float32, least / len(split), top_value / len(split))
        gain = gain * jnp.repeat(jnp.exp(steps), dims[axis_at] // parts).reshape((-1,) + (1,) * (len(dims) - 1 - axis_at))
    return gain


def bell_draw(rng, dims, spread, most, cuts=(), kind=jnp.bfloat16):
    result = spread * jax.random.normal(rng, dims, jnp.float32)
    if cuts:
        result = result * steps_of(rng, dims, cuts, -0.22, 0.18)
    return jnp.clip(result, -most, most).astype(kind)


def setup_inputs(seed: int = 0, part: int = 0) -> dict:
    key_of = jax.random.split(jax.random.key(seed), 9)
    part_splits = jax.random.split(jax.random.fold_in(key_of[8], part), 9)
    return {
        "theta": bell_draw(part_splits[0], (NR, NC), 1.5, 6.0, ((0, 8), (1, 2)), jnp.float32),
        "seed_map": touch_ends((jax.random.randint(part_splits[1], (NR, NC), 0, 3) < 1).astype(jnp.int32), jax.random.fold_in(part_splits[1], 1), 0, 1),
        "target": jnp.clip(1.0 * jax.random.uniform(part_splits[2], (NR, NC), jnp.float32) ** steps_of(part_splits[2], (NR, NC), ((0, 4), (1, 2)), -0.2, 0.2), 0.0, 1.0).astype(jnp.bfloat16),
        "row_taps": bell_draw(key_of[3], (FOCUS, KERNELS, TAPS), TAPS ** -0.5, 0.5),
        "col_taps": bell_draw(key_of[4], (FOCUS, KERNELS, TAPS), TAPS ** -0.5, 0.5),
        "kernel_weight": jnp.clip(jnp.exp(jax.random.uniform(key_of[5], (FOCUS, KERNELS), jnp.float32, math.log(0.05), math.log(0.4))), 0.05, 0.4),
        "cond_index": touch_ends(jax.random.randint(key_of[6], (CONDS,), 0, FOCUS), jax.random.fold_in(key_of[6], 1), 0, FOCUS - 1).astype(jnp.int32),
        "dose": jnp.clip(jnp.exp(math.log(1.4) - 0.6931472 * jax.random.uniform(key_of[7], (CONDS,), jnp.float32) ** steps_of(key_of[7], (CONDS,), ((0, 2),), -0.2, 0.2)), 0.7, 1.4),
    }


seed_shift = 1.5
steepness = 4.0
threshold = 0.3


def correlate(values, kernel_array, padding_pairs, groups):
    return lax.conv_general_dilated(values, kernel_array, (1, 1), padding_pairs, feature_group_count=groups, precision=lax.Precision.HIGHEST)


def barrier_round(values):
    return lax.optimization_barrier(values.astype(jnp.bfloat16)).astype(jnp.float32)


def reference(theta, seed_map, target, row_taps, col_taps, kernel_weight, cond_index, dose):
    sig = jax.nn.sigmoid(theta + seed_shift * (2 * seed_map - 1).astype(jnp.float32))
    mask_value = barrier_round(sig)
    target_value = target.astype(jnp.float32)
    kernel_count = row_taps.shape[1]
    padded = jnp.pad(mask_value, ((0, 0), (HALF, HALF)))

    def one_condition(running, inputs):
        focus_row, dose_val = inputs
        row_tap = row_taps[focus_row].astype(jnp.float32)
        col_tap = col_taps[focus_row].astype(jnp.float32)
        weights = kernel_weight[focus_row]
        row_pass = correlate(padded[None, None], row_tap[:, None, :, None], ((HALF, HALF), (0, 0)), 1)
        row_pass = barrier_round(row_pass)
        field_amp = correlate(row_pass, col_tap[:, None, None, :], ((0, 0), (0, 0)), kernel_count)[0]
        intensity = jnp.sum(weights[:, None, None] * field_amp * field_amp, axis=0)
        resist = jax.nn.sigmoid(steepness * (dose_val * intensity - threshold))
        slope_term = 2.0 * (resist - target_value) * steepness * dose_val * resist * (1.0 - resist)
        dfield = barrier_round(2.0 * weights[:, None, None] * field_amp * slope_term[None])
        dpadded = jnp.pad(dfield, ((0, 0), (HALF, HALF), (0, 0)))
        col_back = correlate(dpadded[None], col_tap[:, ::-1][:, None, None, :], ((0, 0), (HALF, HALF)), kernel_count)
        col_back = barrier_round(col_back)
        grad_part = correlate(col_back, row_tap[:, ::-1][None, :, :, None], ((0, 0), (0, 0)), 1)[0, 0]
        return running + grad_part, None

    start = jnp.zeros(theta.shape, jnp.float32)
    grad_mask, unused = lax.scan(one_condition, start, (cond_index, dose))
    return grad_mask * sig * (1.0 - sig)
```

```python
import functools

import jax
import jax.numpy as jnp
from jax import lax
from jax.experimental import pallas as pl
from jax.experimental.pallas import tpu as pltpu
from jax.sharding import PartitionSpec as P

seed_shift = 1.5
steepness = 4.0
threshold = 0.3
f32 = jnp.float32
bf16 = jnp.bfloat16


def sigmoid(x):
    return 1.0 / (1.0 + jnp.exp(-x))


def toeplitz(row, count, shift):
    wide = jnp.broadcast_to(row, (count, row.shape[1]))
    return pltpu.roll(wide, shift, 1, stride=1, stride_axis=0)


def dot(a, b):
    return jnp.dot(a, b, preferred_element_type=f32)


def body(
    stripes,
    groups,
    cores,
    half,
    theta_in,
    seed_in,
    target_in,
    row_taps_in,
    col_taps_in,
    weight_in,
    cond_in,
    dose_in,
    out_ref,
    theta_ref,
    seed_ref,
    row_taps_ref,
    col_taps_ref,
    weight_ref,
    cond_ref,
    dose_ref,
    load_sem,
    sig_ref,
    own,
    edge,
    full_in,
    edge_in,
    tgt,
    ext,
    taps_pad,
    taps_rev,
    row_fwd,
    row_adj,
    col_fwd,
    col_adj,
    row_pass,
    field,
    col_back,
    grad_full,
    grad_edge,
    part_full,
    part_edge,
    send_full,
    recv_full,
    send_edge,
    recv_edge,
    send_part,
    recv_part,
    send_rim,
    recv_rim,
    send_t,
    recv_t,
    send_c,
    recv_c,
    send_d,
    recv_d,
):
    band = 2 * half
    rows, cols = theta_ref.shape
    foci, kernels, taps = row_taps_ref.shape
    slots = cond_in.shape[0]
    reach = half // rows
    span = 2 * reach + 1
    depth = kernels * rows
    blocks = cols // band
    stripe = lax.axis_index("stripe")
    group = lax.axis_index("cond")
    core = lax.axis_index("col")
    other = cores - 1 - core
    last = stripes * groups
    mine = stripe * groups + group
    work = stripe * groups + groups - 1 - group
    has_up = stripe > 0
    has_down = stripe < stripes - 1
    side = jnp.where(group < groups // 2, -1, 1)

    def inside(at):
        return (at >= 0) & (at < last)

    def split(at):
        up = lax.div(at + groups, groups)
        return up - 1, at + groups - up * groups

    def owner(at, to_core):
        to_stripe, place = split(at)
        return {"stripe": to_stripe, "cond": place, "col": to_core}

    def worker(at, to_core):
        to_stripe, place = split(at)
        return {"stripe": to_stripe, "cond": groups - 1 - place, "col": to_core}

    def peer(group_step, to_core):
        return {"stripe": stripe, "cond": lax.rem(group + group_step, groups), "col": to_core}

    pairs = (
        (theta_in, theta_ref),
        (seed_in, seed_ref),
        (cond_in, cond_ref.at[group]),
        (dose_in, dose_ref.at[group]),
        (row_taps_in, row_taps_ref),
        (col_taps_in, col_taps_ref),
        (weight_in, weight_ref),
    )
    loads = [
        pltpu.make_async_copy(source, into, load_sem.at[i])
        for i, (source, into) in enumerate(pairs)
    ]
    for load in loads:
        load.start()

    barrier = pltpu.get_barrier_semaphore()

    def greet(device):
        pl.semaphore_signal(
            barrier, inc=1, device_id=device, device_id_type=pl.DeviceIdType.MESH
        )

    greeted = groups * cores - 1
    for j in range(groups):
        to_group = lax.rem(group + j, groups)
        skew = jnp.abs(group + to_group - (groups - 1))
        close = jnp.abs(skew - groups) <= reach
        for exists, step in ((has_up, -1), (has_down, 1)):
            linked = exists & close
            greeted = greeted + jnp.where(linked, cores, 0)

            @pl.when(linked)
            def _(to_group=to_group, step=step):
                for c in range(cores):
                    greet({"stripe": stripe + step, "cond": to_group, "col": c})

        if j:
            for c in range(cores):
                greet(peer(j, c))
    greet(peer(0, other))

    loads[0].wait()
    loads[1].wait()
    sig = sigmoid(theta_ref[...] + seed_shift * (2 * seed_ref[...] - 1).astype(f32))
    sig_ref[...] = sig
    turned = pltpu.roll(sig, half, 1).astype(bf16)
    own[...] = turned
    edge[...] = turned[:, 0:band]
    loads[2].wait()
    loads[3].wait()

    pl.semaphore_wait(barrier, greeted)

    def remote(source, target, send, recv, device):
        return pltpu.make_async_remote_copy(
            src_ref=source,
            dst_ref=target,
            send_sem=send,
            recv_sem=recv,
            device_id=device,
            device_id_type=pl.DeviceIdType.MESH,
        )

    def cond_copies(group_step):
        to = peer(group_step, core)
        at = group_step - 1
        return (
            remote(cond_ref.at[group], cond_ref.at[group], send_c.at[at], recv_c.at[at], to),
            remote(dose_ref.at[group], dose_ref.at[group], send_d.at[at], recv_d.at[at], to),
        )

    def cond_arrivals(group_step):
        source = lax.rem(group - group_step + groups, groups)
        to = peer(group_step, core)
        at = group_step - 1
        return (
            remote(cond_ref.at[source], cond_ref.at[source], send_c.at[at], recv_c.at[at], to),
            remote(dose_ref.at[source], dose_ref.at[source], send_d.at[at], recv_d.at[at], to),
        )

    def mask_full(step):
        slot = reach - step
        to = worker(mine + step, other)
        return remote(own, full_in.at[slot], send_full.at[slot], recv_full.at[slot], to)

    def mask_edge(step):
        slot = reach - step
        to = worker(mine + step, core)
        return remote(edge, edge_in.at[slot], send_edge.at[slot], recv_edge.at[slot], to)

    def full_arrival(slot):
        tile = full_in.at[slot]
        return remote(tile, tile, send_full.at[slot], recv_full.at[slot], peer(0, other))

    def edge_arrival(slot):
        tile = edge_in.at[slot]
        return remote(tile, tile, send_edge.at[slot], recv_edge.at[slot], peer(0, other))

    for group_step in range(1, groups):
        for copy in cond_copies(group_step):
            copy.start()

    order = [*range(reach, -reach - 1, -1)]
    for e in order:
        step = side * e

        @pl.when(inside(mine + step) & (mine + step != work))
        def _(step=step):
            mask_edge(step).start()

    for e in order:
        step = side * e

        @pl.when(inside(mine + step))
        def _(step=step):
            mask_full(step).start()

    first_row = pl.multiple_of((groups - 1 - group) * rows, rows)
    target_copy = remote(
        target_in.at[pl.ds(first_row, rows), :], tgt, send_t, recv_t, peer(0, other)
    )
    target_copy.start()

    for slot in range(span):

        @pl.when(work - reach + slot == mine)
        def _(slot=slot):
            edge_in[slot] = edge[...]

        @pl.when(jnp.logical_not(inside(work - reach + slot)))
        def _(slot=slot):
            full_in[slot] = jnp.zeros((rows, cols), bf16)
            edge_in[slot] = jnp.zeros((rows, band), bf16)

        @pl.when(jnp.logical_not(inside(mine - reach + slot)))
        def _(slot=slot):
            part_full[slot] = jnp.zeros((rows, cols), bf16)
            part_edge[slot] = jnp.zeros((rows, band), bf16)

    if span * rows < 2 * band:
        ext[span * rows :, :] = jnp.zeros((2 * band - span * rows, cols + band), bf16)
    taps_pad[...] = jnp.zeros_like(taps_pad)
    mirror = (
        lax.broadcasted_iota(jnp.int32, (2 * band, 2 * band), 0)
        + lax.broadcasted_iota(jnp.int32, (2 * band, 2 * band), 1)
        == band
    ).astype(f32).astype(bf16)
    for load in loads[4:]:
        load.wait()
    for f in range(foci):
        taps_pad[f * 8 : f * 8 + kernels, 0:taps] = row_taps_ref[f].astype(f32)
        taps_pad[(foci + f) * 8 : (foci + f) * 8 + kernels, 0:taps] = col_taps_ref[f].astype(f32)
    taps_rev[...] = dot(taps_pad[...].astype(bf16), mirror)
    per = band // rows
    lane = lax.broadcasted_iota(jnp.int32, (span * rows, band), 1)
    for f in range(foci):
        for k in range(kernels):
            at = f * 8 + k
            row_fwd[f, k * rows : (k + 1) * rows, :] = toeplitz(
                taps_pad[at : at + 1, :], rows, 0
            ).astype(bf16)
        for first in range(0, kernels, per):
            tile = None
            count = min(per, kernels - first)
            for i in range(count):
                at = f * 8 + first + i
                strip = toeplitz(taps_rev[at : at + 1, :], span * rows, band + i * rows)[:, 0:band]
                tile = strip if tile is None else jnp.where(lane < i * rows, tile, strip)
            row_adj[f, :, first * rows : (first + count) * rows] = tile[:, 0 : count * rows].astype(bf16)
        for k in range(kernels):
            at = (foci + f) * 8 + k
            strip = toeplitz(taps_rev[at : at + 1, :], band, 0).astype(bf16)
            col_fwd[f * kernels + k, 0:band, :] = strip[:, band:]
            col_fwd[f * kernels + k, band:, :] = strip[:, 0:band]
            col_adj[f * kernels + k] = toeplitz(taps_pad[at : at + 1, :], band, 0).astype(bf16)

    for group_step in range(1, groups):
        for copy in cond_arrivals(group_step):
            copy.wait_recv()
    for slot in range(span):
        at = work - reach + slot

        @pl.when(inside(at))
        def _(slot=slot):
            full_arrival(slot).wait_recv()

        @pl.when(inside(at) & (at != mine))
        def _(slot=slot):
            edge_arrival(slot).wait_recv()

    lanes = lax.broadcasted_iota(jnp.int32, (rows, band), 1)
    left_half = other == 0
    high = (lanes >= half).astype(f32)
    low = 1.0 - high
    high_16, low_16 = high.astype(bf16), low.astype(bf16)
    before = (low * jnp.where(left_half, 0.0, 1.0)).astype(bf16)
    after = (high * jnp.where(left_half, 1.0, 0.0)).astype(bf16)
    for slot in range(span):
        turned = full_in[slot, :, 0:band]
        rim = edge_in[slot]
        place = slice(slot * rows, (slot + 1) * rows)
        ext[place, 0:band] = turned * high_16 + rim * before
        ext[place, band:cols] = full_in[slot, :, band:]
        ext[place, cols:] = turned * low_16 + rim * after

    conds = [(g, s) for g in range(groups) for s in range(slots)]
    focus = [cond_ref[g, s] for g, s in conds]
    for c in range(len(conds)):
        row_pass[c * depth : (c + 1) * depth, :] = dot(row_fwd[focus[c]], ext[...]).astype(bf16)
    target_copy.wait_recv()
    aim = jnp.concatenate(
        [tgt[:, b * band : (b + 1) * band] for b in range(blocks)], axis=0
    ).astype(f32)
    for c, (g, s) in enumerate(conds):
        dose = dose_ref[g, s]
        intensity = jnp.zeros((blocks * rows, band), f32)
        for k in range(kernels):
            first = c * depth + k * rows
            left = jnp.concatenate(
                [
                    row_pass[first : first + rows, b * band : (b + 2) * band]
                    for b in range(blocks)
                ],
                axis=0,
            )
            amp = dot(left, col_fwd[focus[c] * kernels + k])
            field[c * kernels + k] = amp
            intensity = intensity + weight_ref[focus[c], k] * (amp * amp)
        resist = sigmoid(steepness * (dose * intensity - threshold))
        slope = (2.0 * steepness) * (resist - aim) * dose * resist * (1.0 - resist)
        for k in range(kernels):
            dfield = ((2.0 * weight_ref[focus[c], k]) * field[c * kernels + k] * slope).astype(bf16)
            spread = dot(dfield, col_adj[focus[c] * kernels + k])
            first = c * depth + k * rows
            for b in range(blocks + 1):
                piece = None
                if b < blocks:
                    piece = spread[b * rows : (b + 1) * rows, 0:band]
                if b > 0:
                    more = spread[(b - 1) * rows : b * rows, band:]
                    piece = more if piece is None else piece + more
                col_back[first : first + rows, b * band : (b + 1) * band] = piece.astype(bf16)

    if depth % band == 0:
        total = dot(
            jnp.concatenate([row_adj[focus[c]] for c in range(len(conds))], axis=1), col_back[...]
        )
    else:
        total = jnp.zeros((span * rows, cols + band), f32)
        for c in range(len(conds)):
            total = total + dot(row_adj[focus[c]], col_back[c * depth : (c + 1) * depth, :])

    for slot in range(span):
        rows_of = total[slot * rows : (slot + 1) * rows, :]
        head, tail = rows_of[:, 0:band], rows_of[:, cols:]
        grad_full[slot, :, 0:band] = jnp.where(lanes >= half, head, tail).astype(bf16)
        grad_full[slot, :, band:] = rows_of[:, band:cols].astype(bf16)
        grad_edge[slot] = jnp.where(left_half, tail * high, head * low).astype(bf16)

    def part_copy(slot):
        into = 2 * reach - slot
        to = owner(work - reach + slot, other)
        return remote(
            grad_full.at[slot], part_full.at[into], send_part.at[into], recv_part.at[into], to
        )

    def rim_copy(slot):
        into = 2 * reach - slot
        to = owner(work - reach + slot, core)
        return remote(
            grad_edge.at[slot], part_edge.at[into], send_rim.at[into], recv_rim.at[into], to
        )

    def part_arrival(slot):
        tile = part_full.at[slot]
        return remote(tile, tile, send_part.at[slot], recv_part.at[slot], peer(0, other))

    def rim_arrival(slot):
        tile = part_edge.at[slot]
        return remote(tile, tile, send_rim.at[slot], recv_rim.at[slot], peer(0, other))

    for e in order:
        slot = reach - side * e
        at = work - reach + slot

        @pl.when(inside(at) & (at != mine))
        def _(slot=slot):
            rim_copy(slot).start()

    for e in order:
        slot = reach - side * e

        @pl.when(inside(work - reach + slot))
        def _(slot=slot):
            part_copy(slot).start()

    for slot in range(span):

        @pl.when(work - reach + slot == mine)
        def _(slot=slot):
            part_edge[2 * reach - slot] = grad_edge[slot]

    for slot in range(span):
        at = mine - reach + slot

        @pl.when(inside(at))
        def _(slot=slot):
            part_arrival(slot).wait_recv()

        @pl.when(inside(at) & (at != work))
        def _(slot=slot):
            rim_arrival(slot).wait_recv()

    sums = jnp.zeros((rows, cols), f32)
    rims = jnp.zeros((rows, band), f32)
    for slot in range(span):
        sums = sums + part_full[slot].astype(f32)
        rims = rims + part_edge[slot].astype(f32)
    sums = jnp.concatenate([sums[:, 0:band] + rims, sums[:, band:]], axis=1)
    sig = sig_ref[...]
    out_ref[...] = pltpu.roll(sums, cols - half, 1) * sig * (1.0 - sig)

    for group_step in range(1, groups):
        for copy in cond_copies(group_step):
            copy.wait_send()
    target_copy.wait_send()
    for e in order:
        step = side * e
        slot = reach - side * e
        at = work - reach + slot

        @pl.when(inside(mine + step))
        def _(step=step):
            mask_full(step).wait_send()

        @pl.when(inside(mine + step) & (mine + step != work))
        def _(step=step):
            mask_edge(step).wait_send()

        @pl.when(inside(at))
        def _(slot=slot):
            part_copy(slot).wait_send()

        @pl.when(inside(at) & (at != mine))
        def _(slot=slot):
            rim_copy(slot).wait_send()


def shards(stripes, groups, cores, theta, seed_map, target, row_taps, col_taps, weight, cond_index, dose):
    rows, cols = theta.shape
    foci, kernels, taps = row_taps.shape
    half = taps // 2
    band = 2 * half
    span = 2 * (half // rows) + 1
    slots = cond_index.shape[0]
    conds = groups * slots
    depth = kernels * rows
    wide = cols + band
    hbm = pl.BlockSpec(memory_space=pltpu.HBM)
    vmem = pltpu.VMEM
    dma = pltpu.SemaphoreType.DMA
    return pl.pallas_call(
        functools.partial(body, stripes, groups, cores, half),
        out_shape=jax.ShapeDtypeStruct((rows, cols), f32),
        in_specs=[hbm] * 8,
        out_specs=pl.BlockSpec(memory_space=vmem),
        scratch_shapes=[
            *[vmem(a.shape, a.dtype) for a in (theta, seed_map, row_taps, col_taps)],
            pltpu.SMEM(weight.shape, weight.dtype),
            pltpu.SMEM((groups, slots), cond_index.dtype),
            pltpu.SMEM((groups, slots), dose.dtype),
            dma((7,)),
            vmem((rows, cols), f32),
            vmem((rows, cols), bf16),
            vmem((rows, band), bf16),
            vmem((span, rows, cols), bf16),
            vmem((span, rows, band), bf16),
            vmem((rows, cols), bf16),
            vmem((2 * band, wide), bf16),
            vmem((2 * foci * 8, 2 * band), f32),
            vmem((2 * foci * 8, 2 * band), f32),
            vmem((foci, depth, 2 * band), bf16),
            vmem((foci, span * rows, depth), bf16),
            vmem((foci * kernels, 2 * band, band), bf16),
            vmem((foci * kernels, band, 2 * band), bf16),
            vmem((conds * depth, wide), bf16),
            vmem((conds * kernels, cols // band * rows, band), f32),
            vmem((conds * depth, wide), bf16),
            vmem((span, rows, cols), bf16),
            vmem((span, rows, band), bf16),
            vmem((span, rows, cols), bf16),
            vmem((span, rows, band), bf16),
            *[dma((span,)) for _ in range(8)],
            dma,
            dma,
            *[dma((groups - 1,)) for _ in range(4)],
        ],
        compiler_params=pltpu.CompilerParams(
            collective_id=0, has_side_effects=True, vmem_limit_bytes=40 * 1024 * 1024
        ),
    )(
        *[
            pltpu.with_memory_space_constraint(a, pltpu.HBM)
            for a in (theta, seed_map, target, row_taps, col_taps, weight, cond_index, dose)
        ]
    )


def solution(mesh):
    sizes = [mesh.shape[name] for name in ("stripe", "cond", "col")]
    return jax.shard_map(
        functools.partial(shards, *sizes),
        mesh=mesh,
        in_specs=(
            P(("blocks", "stripe", "cond"), "col"),
            P(("blocks", "stripe", "cond"), "col"),
            P(("blocks", "stripe"), "col"),
            P(),
            P(),
            P(),
            P("cond"),
            P("cond"),
        ),
        out_specs=P(("blocks", "stripe", "cond"), "col"),
        check_vma=False,
    )
```

```python
import functools

import jax
import jax.numpy as jnp
from jax import lax
from jax.experimental import pallas as pl
from jax.experimental.pallas import tpu as pltpu
from jax.sharding import PartitionSpec as P

seed_shift = 1.5
steepness = 4.0
threshold = 0.3
f32 = jnp.float32
bf16 = jnp.bfloat16


def sigmoid(x):
    return 1.0 / (1.0 + jnp.exp(-x))


def toeplitz(row, count, shift):
    wide = jnp.broadcast_to(row, (count, row.shape[1]))
    return pltpu.roll(wide, shift, 1, stride=1, stride_axis=0)


def dot(a, b):
    return jnp.dot(a, b, preferred_element_type=f32)


def body(
    stripes,
    groups,
    cores,
    half,
    theta_in,
    seed_in,
    target_in,
    row_taps_in,
    col_taps_in,
    weight_in,
    cond_in,
    dose_in,
    out_ref,
    theta_ref,
    seed_ref,
    row_taps_ref,
    col_taps_ref,
    weight_ref,
    cond_ref,
    dose_ref,
    load_sem,
    sig_ref,
    own,
    edge,
    full_in,
    edge_in,
    tgt,
    ext,
    taps_pad,
    taps_rev,
    row_fwd,
    row_adj,
    col_fwd,
    row_pass,
    field,
    col_back,
    grad_full,
    grad_edge,
    part_full,
    part_edge,
    send_full,
    recv_full,
    send_edge,
    recv_edge,
    send_part,
    recv_part,
    send_rim,
    recv_rim,
    send_t,
    recv_t,
    send_c,
    recv_c,
    send_d,
    recv_d,
):
    band = 2 * half
    rows, cols = theta_ref.shape
    foci, kernels, taps = row_taps_ref.shape
    slots = cond_in.shape[0]
    reach = half // rows
    span = 2 * reach + 1
    depth = kernels * rows
    blocks = cols // band
    stripe = lax.axis_index("stripe")
    group = lax.axis_index("cond")
    core = lax.axis_index("col")
    other = cores - 1 - core
    last = stripes * groups
    mine = stripe * groups + group
    work = stripe * groups + groups - 1 - group
    side = jnp.where(group < groups // 2, -1, 1)

    def inside(at):
        return (at >= 0) & (at < last)

    def split(at):
        up = lax.div(at + groups, groups)
        return up - 1, at + groups - up * groups

    def owner(at, to_core):
        to_stripe, place = split(at)
        return {"stripe": to_stripe, "cond": place, "col": to_core}

    def worker(at, to_core):
        to_stripe, place = split(at)
        return {"stripe": to_stripe, "cond": groups - 1 - place, "col": to_core}

    def peer(group_step, to_core):
        return {"stripe": stripe, "cond": lax.rem(group + group_step, groups), "col": to_core}

    pairs = (
        (theta_in, theta_ref),
        (seed_in, seed_ref),
        (cond_in, cond_ref.at[group]),
        (dose_in, dose_ref.at[group]),
        (row_taps_in, row_taps_ref),
        (col_taps_in, col_taps_ref),
        (weight_in, weight_ref),
    )
    loads = [
        pltpu.make_async_copy(source, into, load_sem.at[i])
        for i, (source, into) in enumerate(pairs)
    ]
    for load in loads:
        load.start()

    barrier = pltpu.get_barrier_semaphore()

    def greet(device):
        pl.semaphore_signal(
            barrier, inc=1, device_id=device, device_id_type=pl.DeviceIdType.MESH
        )

    greeted = 1 + groups - 1
    for d in range(-reach, reach + 1):
        source, target = work + d, mine + d
        source_place, target_place = split(source), split(target)
        here = source_place[0] == stripe
        greeted = greeted + jnp.where(
            inside(target), jnp.where(target_place[0] != stripe, cores, 0), 0
        )
        greeted = greeted + jnp.where(
            (target_place[0] == stripe) & (groups - 1 - target_place[1] != group), cores - 1, 0
        )

        @pl.when(inside(source) & jnp.logical_not(here))
        def _(source=source):
            for c in range(cores):
                greet(owner(source, c))

        @pl.when(here & (source != mine))
        def _(source=source):
            greet(owner(source, other))

    for j in range(1, groups):
        greet(peer(j, core))
    greet(peer(0, other))

    loads[0].wait()
    loads[1].wait()
    sig = sigmoid(theta_ref[...] + seed_shift * (2 * seed_ref[...] - 1).astype(f32))
    sig_ref[...] = sig
    turned = pltpu.roll(sig, half, 1).astype(bf16)
    own[...] = turned
    edge[...] = turned[:, 0:band]
    loads[2].wait()
    loads[3].wait()

    pl.semaphore_wait(barrier, greeted)

    def remote(source, target, send, recv, device):
        return pltpu.make_async_remote_copy(
            src_ref=source,
            dst_ref=target,
            send_sem=send,
            recv_sem=recv,
            device_id=device,
            device_id_type=pl.DeviceIdType.MESH,
        )

    def cond_copies(group_step):
        to = peer(group_step, core)
        at = group_step - 1
        return (
            remote(cond_ref.at[group], cond_ref.at[group], send_c.at[at], recv_c.at[at], to),
            remote(dose_ref.at[group], dose_ref.at[group], send_d.at[at], recv_d.at[at], to),
        )

    def cond_arrivals(group_step):
        source = lax.rem(group - group_step + groups, groups)
        to = peer(group_step, core)
        at = group_step - 1
        return (
            remote(cond_ref.at[source], cond_ref.at[source], send_c.at[at], recv_c.at[at], to),
            remote(dose_ref.at[source], dose_ref.at[source], send_d.at[at], recv_d.at[at], to),
        )

    def mask_full(step):
        slot = reach - step
        to = worker(mine + step, other)
        return remote(own, full_in.at[slot], send_full.at[slot], recv_full.at[slot], to)

    def mask_edge(step):
        slot = reach - step
        to = worker(mine + step, core)
        return remote(edge, edge_in.at[slot], send_edge.at[slot], recv_edge.at[slot], to)

    def full_arrival(slot):
        tile = full_in.at[slot]
        return remote(tile, tile, send_full.at[slot], recv_full.at[slot], peer(0, other))

    def edge_arrival(slot):
        tile = edge_in.at[slot]
        return remote(tile, tile, send_edge.at[slot], recv_edge.at[slot], peer(0, other))

    for group_step in range(1, groups):
        for copy in cond_copies(group_step):
            copy.start()

    order = [*range(reach, -reach - 1, -1)]
    for e in order:
        step = side * e

        @pl.when(inside(mine + step) & (mine + step != work))
        def _(step=step):
            mask_edge(step).start()

    for e in order:
        step = side * e

        @pl.when(inside(mine + step))
        def _(step=step):
            mask_full(step).start()

    first_row = pl.multiple_of((groups - 1 - group) * rows, rows)
    target_copy = remote(
        target_in.at[pl.ds(first_row, rows), :], tgt, send_t, recv_t, peer(0, other)
    )
    target_copy.start()

    for slot in range(span):

        @pl.when(work - reach + slot == mine)
        def _(slot=slot):
            edge_in[slot] = edge[...]

        @pl.when(jnp.logical_not(inside(work - reach + slot)))
        def _(slot=slot):
            full_in[slot] = jnp.zeros((rows, cols), bf16)
            edge_in[slot] = jnp.zeros((rows, band), bf16)

        @pl.when(jnp.logical_not(inside(mine - reach + slot)))
        def _(slot=slot):
            part_full[slot] = jnp.zeros((rows, cols), bf16)
            part_edge[slot] = jnp.zeros((rows, band), bf16)

    if span * rows < 2 * band:
        ext[span * rows :, :] = jnp.zeros((2 * band - span * rows, cols + band), bf16)
    taps_pad[...] = jnp.zeros_like(taps_pad)
    mirror = (
        lax.broadcasted_iota(jnp.int32, (2 * band, 2 * band), 0)
        + lax.broadcasted_iota(jnp.int32, (2 * band, 2 * band), 1)
        == band
    ).astype(f32).astype(bf16)
    for load in loads[4:]:
        load.wait()
    for f in range(foci):
        taps_pad[f * 8 : f * 8 + kernels, 0:taps] = row_taps_ref[f].astype(f32)
        taps_pad[(foci + f) * 8 : (foci + f) * 8 + kernels, 0:taps] = col_taps_ref[f].astype(f32)
    taps_rev[...] = dot(taps_pad[...].astype(bf16), mirror)
    per = band // rows
    lane = lax.broadcasted_iota(jnp.int32, (span * rows, band), 1)
    for f in range(foci):
        for k in range(kernels):
            at = f * 8 + k
            row_fwd[f, k * rows : (k + 1) * rows, :] = toeplitz(
                taps_pad[at : at + 1, :], rows, 0
            ).astype(bf16)
        for first in range(0, kernels, per):
            tile = None
            count = min(per, kernels - first)
            for i in range(count):
                at = f * 8 + first + i
                strip = toeplitz(taps_rev[at : at + 1, :], span * rows, band + i * rows)[:, 0:band]
                tile = strip if tile is None else jnp.where(lane < i * rows, tile, strip)
            row_adj[f, :, first * rows : (first + count) * rows] = tile[:, 0 : count * rows].astype(bf16)
        for k in range(kernels):
            at = (foci + f) * 8 + k
            strip = toeplitz(taps_rev[at : at + 1, :], band, 0).astype(bf16)
            col_fwd[f * kernels + k, 0:band, :] = strip[:, band:]
            col_fwd[f * kernels + k, band:, :] = strip[:, 0:band]

    for group_step in range(1, groups):
        for copy in cond_arrivals(group_step):
            copy.wait_recv()
    for slot in range(span):
        at = work - reach + slot

        @pl.when(inside(at))
        def _(slot=slot):
            full_arrival(slot).wait_recv()

        @pl.when(inside(at) & (at != mine))
        def _(slot=slot):
            edge_arrival(slot).wait_recv()

    lanes = lax.broadcasted_iota(jnp.int32, (rows, band), 1)
    left_half = other == 0
    high = (lanes >= half).astype(f32)
    low = 1.0 - high
    high_16, low_16 = high.astype(bf16), low.astype(bf16)
    before = (low * jnp.where(left_half, 0.0, 1.0)).astype(bf16)
    after = (high * jnp.where(left_half, 1.0, 0.0)).astype(bf16)
    for slot in range(span):
        turned = full_in[slot, :, 0:band]
        rim = edge_in[slot]
        place = slice(slot * rows, (slot + 1) * rows)
        ext[place, 0:band] = turned * high_16 + rim * before
        ext[place, band:cols] = full_in[slot, :, band:]
        ext[place, cols:] = turned * low_16 + rim * after

    conds = [(g, s) for g in range(groups) for s in range(slots)]
    focus = [cond_ref[g, s] for g, s in conds]
    for c in range(len(conds)):
        row_pass[c * depth : (c + 1) * depth, :] = dot(row_fwd[focus[c]], ext[...]).astype(bf16)
    target_copy.wait_recv()
    aim = jnp.concatenate(
        [tgt[:, b * band : (b + 1) * band] for b in range(blocks)], axis=0
    ).astype(f32)
    slopes = []
    for c in range(len(conds)):
        intensity = jnp.zeros((blocks * rows, band), f32)
        for k in range(kernels):
            first = c * depth + k * rows
            left = jnp.concatenate(
                [
                    row_pass[first : first + rows, b * band : (b + 2) * band]
                    for b in range(blocks)
                ],
                axis=0,
            )
            amp = dot(left, col_fwd[focus[c] * kernels + k])
            field[c * kernels + k] = amp
            intensity = intensity + weight_ref[focus[c], k] * (amp * amp)
        slopes.append(intensity)
    for c, (g, s) in enumerate(conds):
        dose = dose_ref[g, s]
        resist = sigmoid(steepness * (dose * slopes[c] - threshold))
        slopes[c] = (2.0 * steepness) * (resist - aim) * dose * resist * (1.0 - resist)
    for c in range(len(conds)):
        for k in range(kernels):
            weight = 2.0 * weight_ref[focus[c], k]
            dfield = (weight * field[c * kernels + k] * slopes[c]).astype(bf16)
            spread = lax.dot_general(
                dfield,
                col_fwd[focus[c] * kernels + k],
                (((1,), (1,)), ((), ())),
                preferred_element_type=f32,
            )
            first = c * depth + k * rows
            for b in range(blocks + 1):
                piece = None
                if b < blocks:
                    piece = spread[b * rows : (b + 1) * rows, 0:band]
                if b > 0:
                    more = spread[(b - 1) * rows : b * rows, band:]
                    piece = more if piece is None else piece + more
                col_back[first : first + rows, b * band : (b + 1) * band] = piece.astype(bf16)

    if depth % band == 0:
        total = dot(
            jnp.concatenate([row_adj[focus[c]] for c in range(len(conds))], axis=1), col_back[...]
        )
    else:
        total = jnp.zeros((span * rows, cols + band), f32)
        for c in range(len(conds)):
            total = total + dot(row_adj[focus[c]], col_back[c * depth : (c + 1) * depth, :])

    for slot in range(span):
        rows_of = total[slot * rows : (slot + 1) * rows, :]
        head, tail = rows_of[:, 0:band], rows_of[:, cols:]
        grad_full[slot, :, 0:band] = jnp.where(lanes >= half, head, tail).astype(bf16)
        grad_full[slot, :, band:] = rows_of[:, band:cols].astype(bf16)
        grad_edge[slot] = jnp.where(left_half, tail * high, head * low).astype(bf16)

    def part_copy(slot):
        into = 2 * reach - slot
        to = owner(work - reach + slot, other)
        return remote(
            grad_full.at[slot], part_full.at[into], send_part.at[into], recv_part.at[into], to
        )

    def rim_copy(slot):
        into = 2 * reach - slot
        to = owner(work - reach + slot, core)
        return remote(
            grad_edge.at[slot], part_edge.at[into], send_rim.at[into], recv_rim.at[into], to
        )

    def part_arrival(slot):
        tile = part_full.at[slot]
        return remote(tile, tile, send_part.at[slot], recv_part.at[slot], peer(0, other))

    def rim_arrival(slot):
        tile = part_edge.at[slot]
        return remote(tile, tile, send_rim.at[slot], recv_rim.at[slot], peer(0, other))

    for e in order:
        slot = reach - side * e
        at = work - reach + slot

        @pl.when(inside(at) & (at != mine))
        def _(slot=slot):
            rim_copy(slot).start()

    for e in order:
        slot = reach - side * e

        @pl.when(inside(work - reach + slot))
        def _(slot=slot):
            part_copy(slot).start()

    for slot in range(span):

        @pl.when(work - reach + slot == mine)
        def _(slot=slot):
            part_edge[2 * reach - slot] = grad_edge[slot]

    for slot in range(span):
        at = mine - reach + slot

        @pl.when(inside(at))
        def _(slot=slot):
            part_arrival(slot).wait_recv()

        @pl.when(inside(at) & (at != work))
        def _(slot=slot):
            rim_arrival(slot).wait_recv()

    sums = jnp.zeros((rows, cols), f32)
    rims = jnp.zeros((rows, band), f32)
    for slot in range(span):
        sums = sums + part_full[slot].astype(f32)
        rims = rims + part_edge[slot].astype(f32)
    sums = jnp.concatenate([sums[:, 0:band] + rims, sums[:, band:]], axis=1)
    sig = sig_ref[...]
    out_ref[...] = pltpu.roll(sums, cols - half, 1) * sig * (1.0 - sig)

    for group_step in range(1, groups):
        for copy in cond_copies(group_step):
            copy.wait_send()
    target_copy.wait_send()
    for e in order:
        step = side * e
        slot = reach - side * e
        at = work - reach + slot

        @pl.when(inside(mine + step))
        def _(step=step):
            mask_full(step).wait_send()

        @pl.when(inside(mine + step) & (mine + step != work))
        def _(step=step):
            mask_edge(step).wait_send()

        @pl.when(inside(at))
        def _(slot=slot):
            part_copy(slot).wait_send()

        @pl.when(inside(at) & (at != mine))
        def _(slot=slot):
            rim_copy(slot).wait_send()


def shards(stripes, groups, cores, theta, seed_map, target, row_taps, col_taps, weight, cond_index, dose):
    rows, cols = theta.shape
    foci, kernels, taps = row_taps.shape
    half = taps // 2
    band = 2 * half
    span = 2 * (half // rows) + 1
    slots = cond_index.shape[0]
    conds = groups * slots
    depth = kernels * rows
    wide = cols + band
    hbm = pl.BlockSpec(memory_space=pltpu.HBM)
    vmem = pltpu.VMEM
    dma = pltpu.SemaphoreType.DMA
    return pl.pallas_call(
        functools.partial(body, stripes, groups, cores, half),
        out_shape=jax.ShapeDtypeStruct((rows, cols), f32),
        in_specs=[hbm] * 8,
        out_specs=pl.BlockSpec(memory_space=vmem),
        scratch_shapes=[
            *[vmem(a.shape, a.dtype) for a in (theta, seed_map, row_taps, col_taps)],
            pltpu.SMEM(weight.shape, weight.dtype),
            pltpu.SMEM((groups, slots), cond_index.dtype),
            pltpu.SMEM((groups, slots), dose.dtype),
            dma((7,)),
            vmem((rows, cols), f32),
            vmem((rows, cols), bf16),
            vmem((rows, band), bf16),
            vmem((span, rows, cols), bf16),
            vmem((span, rows, band), bf16),
            vmem((rows, cols), bf16),
            vmem((2 * band, wide), bf16),
            vmem((2 * foci * 8, 2 * band), f32),
            vmem((2 * foci * 8, 2 * band), f32),
            vmem((foci, depth, 2 * band), bf16),
            vmem((foci, span * rows, depth), bf16),
            vmem((foci * kernels, 2 * band, band), bf16),
            vmem((conds * depth, wide), bf16),
            vmem((conds * kernels, cols // band * rows, band), f32),
            vmem((conds * depth, wide), bf16),
            vmem((span, rows, cols), bf16),
            vmem((span, rows, band), bf16),
            vmem((span, rows, cols), bf16),
            vmem((span, rows, band), bf16),
            *[dma((span,)) for _ in range(8)],
            dma,
            dma,
            *[dma((groups - 1,)) for _ in range(4)],
        ],
        compiler_params=pltpu.CompilerParams(
            collective_id=0, has_side_effects=True, vmem_limit_bytes=40 * 1024 * 1024
        ),
    )(
        *[
            pltpu.with_memory_space_constraint(a, pltpu.HBM)
            for a in (theta, seed_map, target, row_taps, col_taps, weight, cond_index, dose)
        ]
    )


def solution(mesh):
    sizes = [mesh.shape[name] for name in ("stripe", "cond", "col")]
    return jax.shard_map(
        functools.partial(shards, *sizes),
        mesh=mesh,
        in_specs=(
            P(("blocks", "stripe", "cond"), "col"),
            P(("blocks", "stripe", "cond"), "col"),
            P(("blocks", "stripe"), "col"),
            P(),
            P(),
            P(),
            P("cond"),
            P("cond"),
        ),
        out_specs=P(("blocks", "stripe", "cond"), "col"),
        check_vma=False,
    )
```

```python
import functools

import jax
import jax.numpy as jnp
from jax import lax
from jax.experimental import pallas as pl
from jax.experimental.pallas import tpu as pltpu
from jax.sharding import PartitionSpec as P

seed_shift = 1.5
steepness = 4.0
threshold = 0.3
f32 = jnp.float32
bf16 = jnp.bfloat16


def sigmoid(x):
    return 1.0 / (1.0 + jnp.exp(-x))


def toeplitz(row, count, shift):
    wide = jnp.broadcast_to(row, (count, row.shape[1]))
    return pltpu.roll(wide, shift, 1, stride=1, stride_axis=0)


def dot(a, b):
    return jnp.dot(a, b, preferred_element_type=f32)


def body(
    stripes,
    groups,
    cores,
    half,
    theta_in,
    seed_in,
    target_in,
    row_taps_in,
    col_taps_in,
    weight_in,
    cond_in,
    dose_in,
    out_ref,
    theta_ref,
    seed_ref,
    row_taps_ref,
    col_taps_ref,
    weight_ref,
    cond_ref,
    dose_ref,
    load_sem,
    sig_ref,
    head,
    middle,
    head_in,
    middle_in,
    edge_in,
    tgt,
    ext_ends,
    ext_middle,
    taps_pad,
    taps_rev,
    row_fwd,
    row_adj,
    col_fwd,
    row_pass,
    field,
    back_ends,
    back_middle,
    grad_head,
    grad_middle,
    grad_edge,
    part_head,
    part_middle,
    part_edge,
    mask_sems,
    grad_sems,
    send_t,
    recv_t,
    send_c,
    recv_c,
    send_d,
    recv_d,
):
    band = 2 * half
    rows, cols = theta_ref.shape
    foci, kernels, taps = row_taps_ref.shape
    slots = cond_in.shape[0]
    reach = half // rows
    span = 2 * reach + 1
    depth = kernels * rows
    blocks = cols // band
    stripe = lax.axis_index("stripe")
    group = lax.axis_index("cond")
    core = lax.axis_index("col")
    other = cores - 1 - core
    last = stripes * groups
    mine = stripe * groups + group
    work = stripe * groups + groups - 1 - group
    side = jnp.where(group < groups // 2, -1, 1)

    def inside(at):
        return (at >= 0) & (at < last)

    def split(at):
        up = lax.div(at + groups, groups)
        return up - 1, at + groups - up * groups

    def owner(at, to_core):
        to_stripe, place = split(at)
        return {"stripe": to_stripe, "cond": place, "col": to_core}

    def worker(at, to_core):
        to_stripe, place = split(at)
        return {"stripe": to_stripe, "cond": groups - 1 - place, "col": to_core}

    def peer(group_step, to_core):
        return {"stripe": stripe, "cond": lax.rem(group + group_step, groups), "col": to_core}

    pairs = (
        (theta_in, theta_ref),
        (seed_in, seed_ref),
        (cond_in, cond_ref.at[group]),
        (dose_in, dose_ref.at[group]),
        (row_taps_in, row_taps_ref),
        (col_taps_in, col_taps_ref),
        (weight_in, weight_ref),
    )
    loads = [
        pltpu.make_async_copy(source, into, load_sem.at[i])
        for i, (source, into) in enumerate(pairs)
    ]
    for load in loads[:2]:
        load.start()
    barrier = pltpu.get_barrier_semaphore()

    def greet(device):
        pl.semaphore_signal(
            barrier, inc=1, device_id=device, device_id_type=pl.DeviceIdType.MESH
        )

    greeted = 1 + groups - 1
    for d in range(-reach, reach + 1):
        source, target = work + d, mine + d
        source_place, target_place = split(source), split(target)
        here = source_place[0] == stripe
        greeted = greeted + jnp.where(
            inside(target), jnp.where(target_place[0] != stripe, cores, 0), 0
        )
        greeted = greeted + jnp.where(
            (target_place[0] == stripe) & (groups - 1 - target_place[1] != group), cores - 1, 0
        )

        @pl.when(inside(source) & jnp.logical_not(here))
        def _(source=source):
            for c in range(cores):
                greet(owner(source, c))

        @pl.when(here & (source != mine))
        def _(source=source):
            greet(owner(source, other))

    for j in range(1, groups):
        greet(peer(j, core))
    greet(peer(0, other))
    for load in loads[2:]:
        load.start()

    loads[0].wait()
    loads[1].wait()
    sig = sigmoid(theta_ref[...] + seed_shift * (2 * seed_ref[...] - 1).astype(f32))
    sig_ref[...] = sig
    turned = pltpu.roll(sig, half, 1).astype(bf16)
    head[...] = turned[:, 0:band]
    middle[...] = turned[:, band:]
    loads[2].wait()
    loads[3].wait()

    pl.semaphore_wait(barrier, greeted)

    def remote(source, target, send, recv, device):
        return pltpu.make_async_remote_copy(
            src_ref=source,
            dst_ref=target,
            send_sem=send,
            recv_sem=recv,
            device_id=device,
            device_id_type=pl.DeviceIdType.MESH,
        )

    def cond_copies(group_step):
        to = peer(group_step, core)
        at = group_step - 1
        return (
            remote(cond_ref.at[group], cond_ref.at[group], send_c.at[at], recv_c.at[at], to),
            remote(dose_ref.at[group], dose_ref.at[group], send_d.at[at], recv_d.at[at], to),
        )

    def cond_arrivals(group_step):
        source = lax.rem(group - group_step + groups, groups)
        to = peer(group_step, core)
        at = group_step - 1
        return (
            remote(cond_ref.at[source], cond_ref.at[source], send_c.at[at], recv_c.at[at], to),
            remote(dose_ref.at[source], dose_ref.at[source], send_d.at[at], recv_d.at[at], to),
        )

    def mask_copy(which, step):
        slot = reach - step
        source, into = ((head, edge_in), (head, head_in), (middle, middle_in))[which]
        to = worker(mine + step, other if which else core)
        return remote(
            source, into.at[slot], mask_sems.at[0, which, slot], mask_sems.at[1, which, slot], to
        )

    def mask_arrival(which, slot):
        tile = (edge_in, head_in, middle_in)[which].at[slot]
        return remote(
            tile, tile, mask_sems.at[0, which, slot], mask_sems.at[1, which, slot], peer(0, other)
        )

    def apart(which, at, place):
        return inside(at) if which else inside(at) & (at != place)

    for group_step in range(1, groups):
        for copy in cond_copies(group_step):
            copy.start()

    order = sorted(range(-reach, reach + 1), key=abs)
    for which in range(3):
        for e in order:
            step = side * e

            @pl.when(apart(which, mine + step, work))
            def _(which=which, step=step):
                mask_copy(which, step).start()

    first_row = pl.multiple_of((groups - 1 - group) * rows, rows)
    target_copy = remote(
        target_in.at[pl.ds(first_row, rows), :], tgt, send_t, recv_t, peer(0, other)
    )
    target_copy.start()

    for slot in range(span):

        @pl.when(work - reach + slot == mine)
        def _(slot=slot):
            edge_in[slot] = head[...]

        @pl.when(jnp.logical_not(inside(work - reach + slot)))
        def _(slot=slot):
            head_in[slot] = jnp.zeros((rows, band), bf16)
            middle_in[slot] = jnp.zeros((rows, cols - band), bf16)
            edge_in[slot] = jnp.zeros((rows, band), bf16)

        @pl.when(jnp.logical_not(inside(mine - reach + slot)))
        def _(slot=slot):
            part_head[slot] = jnp.zeros((rows, band), bf16)
            part_middle[slot] = jnp.zeros((rows, cols - band), bf16)
            part_edge[slot] = jnp.zeros((rows, band), bf16)

    if span * rows < 2 * band:
        blank = 2 * band - span * rows
        ext_ends[span * rows :, :] = jnp.zeros((blank, 2 * band), bf16)
        ext_middle[span * rows :, :] = jnp.zeros((blank, cols - band), bf16)
    taps_pad[...] = jnp.zeros_like(taps_pad)
    mirror = (
        lax.broadcasted_iota(jnp.int32, (2 * band, 2 * band), 0)
        + lax.broadcasted_iota(jnp.int32, (2 * band, 2 * band), 1)
        == band
    ).astype(f32).astype(bf16)
    for load in loads[4:]:
        load.wait()
    for f in range(foci):
        taps_pad[f * 8 : f * 8 + kernels, 0:taps] = row_taps_ref[f].astype(f32)
        taps_pad[(foci + f) * 8 : (foci + f) * 8 + kernels, 0:taps] = col_taps_ref[f].astype(f32)
    taps_rev[...] = dot(taps_pad[...].astype(bf16), mirror)
    per = band // rows
    lane = lax.broadcasted_iota(jnp.int32, (span * rows, band), 1)
    for f in range(foci):
        for k in range(kernels):
            at = f * 8 + k
            row_fwd[f, k * rows : (k + 1) * rows, :] = toeplitz(
                taps_pad[at : at + 1, :], rows, 0
            ).astype(bf16)
        for first in range(0, kernels, per):
            tile = None
            count = min(per, kernels - first)
            for i in range(count):
                at = f * 8 + first + i
                strip = toeplitz(taps_rev[at : at + 1, :], span * rows, band + i * rows)[:, 0:band]
                tile = strip if tile is None else jnp.where(lane < i * rows, tile, strip)
            row_adj[f, :, first * rows : (first + count) * rows] = tile[:, 0 : count * rows].astype(bf16)
        for k in range(kernels):
            at = (foci + f) * 8 + k
            strip = toeplitz(taps_rev[at : at + 1, :], band, 0).astype(bf16)
            col_fwd[f * kernels + k, 0:band, :] = strip[:, band:]
            col_fwd[f * kernels + k, band:, :] = strip[:, 0:band]

    for group_step in range(1, groups):
        for copy in cond_arrivals(group_step):
            copy.wait_recv()
    def arrive(which):
        for slot in range(span):

            @pl.when(apart(which, work - reach + slot, mine))
            def _(slot=slot):
                mask_arrival(which, slot).wait_recv()

    arrive(0)
    arrive(1)
    lanes = lax.broadcasted_iota(jnp.int32, (rows, band), 1)
    left_half = other == 0
    high = (lanes >= half).astype(f32)
    low = 1.0 - high
    high_16, low_16 = high.astype(bf16), low.astype(bf16)
    before = (low * jnp.where(left_half, 0.0, 1.0)).astype(bf16)
    after = (high * jnp.where(left_half, 1.0, 0.0)).astype(bf16)
    for slot in range(span):
        turned, rim = head_in[slot], edge_in[slot]
        place = slice(slot * rows, (slot + 1) * rows)
        ext_ends[place, 0:band] = turned * high_16 + rim * before
        ext_ends[place, band:] = turned * low_16 + rim * after

    conds = [(g, s) for g in range(groups) for s in range(slots)]
    focus = [cond_ref[g, s] for g, s in conds]
    for c in range(len(conds)):
        place = slice(c * depth, (c + 1) * depth)
        ends = dot(row_fwd[focus[c]], ext_ends[...]).astype(bf16)
        row_pass[place, 0:band] = ends[:, 0:band]
        row_pass[place, cols:] = ends[:, band:]
    arrive(2)
    for slot in range(span):
        ext_middle[slot * rows : (slot + 1) * rows, :] = middle_in[slot]
    for c in range(len(conds)):
        place = slice(c * depth, (c + 1) * depth)
        row_pass[place, band:cols] = dot(row_fwd[focus[c]], ext_middle[...]).astype(bf16)
    target_copy.wait_recv()
    aim = jnp.concatenate(
        [tgt[:, b * band : (b + 1) * band] for b in range(blocks)], axis=0
    ).astype(f32)
    slopes = []
    for c in range(len(conds)):
        intensity = jnp.zeros((blocks * rows, band), f32)
        for k in range(kernels):
            first = c * depth + k * rows
            left = jnp.concatenate(
                [
                    row_pass[first : first + rows, b * band : (b + 2) * band]
                    for b in range(blocks)
                ],
                axis=0,
            )
            amp = dot(left, col_fwd[focus[c] * kernels + k])
            field[c * kernels + k] = amp
            intensity = intensity + weight_ref[focus[c], k] * (amp * amp)
        slopes.append(intensity)
    for c, (g, s) in enumerate(conds):
        dose = dose_ref[g, s]
        resist = sigmoid(steepness * (dose * slopes[c] - threshold))
        slopes[c] = (2.0 * steepness) * (resist - aim) * dose * resist * (1.0 - resist)
    for c in range(len(conds)):
        for k in range(kernels):
            weight = 2.0 * weight_ref[focus[c], k]
            dfield = (weight * field[c * kernels + k] * slopes[c]).astype(bf16)
            spread = lax.dot_general(
                dfield,
                col_fwd[focus[c] * kernels + k],
                (((1,), (1,)), ((), ())),
                preferred_element_type=f32,
            )
            first = c * depth + k * rows
            for b in range(blocks + 1):
                piece = None
                if b < blocks:
                    piece = spread[b * rows : (b + 1) * rows, 0:band]
                if b > 0:
                    more = spread[(b - 1) * rows : b * rows, band:]
                    piece = more if piece is None else piece + more
                into, at = (back_ends, min(b, 1)) if b in (0, blocks) else (back_middle, b - 1)
                into[first : first + rows, at * band : (at + 1) * band] = piece.astype(bf16)

    def grad_copy(which, slot):
        at = 2 * reach - slot
        source, into = (
            (grad_edge, part_edge),
            (grad_head, part_head),
            (grad_middle, part_middle),
        )[which]
        to = owner(work - reach + slot, other if which else core)
        return remote(
            source.at[slot], into.at[at], grad_sems.at[0, which, at], grad_sems.at[1, which, at], to
        )

    def grad_arrival(which, slot):
        tile = (part_edge, part_head, part_middle)[which].at[slot]
        return remote(
            tile, tile, grad_sems.at[0, which, slot], grad_sems.at[1, which, slot], peer(0, other)
        )

    def send_back(which):
        for e in order:
            slot = reach - side * e

            @pl.when(apart(which, work - reach + slot, mine))
            def _(slot=slot):
                grad_copy(which, slot).start()

    def row_back(right):
        if depth % band == 0:
            left = jnp.concatenate([row_adj[focus[c]] for c in range(len(conds))], axis=1)
            return dot(left, right[...])
        total = jnp.zeros((span * rows, right.shape[1]), f32)
        for c in range(len(conds)):
            total = total + dot(row_adj[focus[c]], right[c * depth : (c + 1) * depth, :])
        return total

    ends = row_back(back_ends)
    for slot in range(span):
        first, final = ends[slot * rows : (slot + 1) * rows, 0:band], ends[slot * rows : (slot + 1) * rows, band:]
        grad_edge[slot] = jnp.where(left_half, final * high, first * low).astype(bf16)
        grad_head[slot] = jnp.where(lanes >= half, first, final).astype(bf16)
    send_back(0)
    send_back(1)
    centre = row_back(back_middle).astype(bf16)
    for slot in range(span):
        grad_middle[slot] = centre[slot * rows : (slot + 1) * rows, :]
    send_back(2)

    for slot in range(span):

        @pl.when(work - reach + slot == mine)
        def _(slot=slot):
            part_edge[2 * reach - slot] = grad_edge[slot]

    sums = []
    for which in range(3):
        for slot in range(span):

            @pl.when(apart(which, mine - reach + slot, work))
            def _(which=which, slot=slot):
                grad_arrival(which, slot).wait_recv()

        part = (part_edge, part_head, part_middle)[which]
        total = part[0].astype(f32)
        for slot in range(1, span):
            total = total + part[slot].astype(f32)
        sums.append(total)
    sums = jnp.concatenate([sums[0] + sums[1], sums[2]], axis=1)
    sig = sig_ref[...]
    out_ref[...] = pltpu.roll(sums, cols - half, 1) * sig * (1.0 - sig)

    for group_step in range(1, groups):
        for copy in cond_copies(group_step):
            copy.wait_send()
    target_copy.wait_send()
    for which in range(3):
        for e in order:
            step = side * e
            slot = reach - step

            @pl.when(apart(which, mine + step, work))
            def _(which=which, step=step):
                mask_copy(which, step).wait_send()

            @pl.when(apart(which, work - reach + slot, mine))
            def _(which=which, slot=slot):
                grad_copy(which, slot).wait_send()


def shards(stripes, groups, cores, theta, seed_map, target, row_taps, col_taps, weight, cond_index, dose):
    rows, cols = theta.shape
    foci, kernels, taps = row_taps.shape
    half = taps // 2
    band = 2 * half
    span = 2 * (half // rows) + 1
    slots = cond_index.shape[0]
    conds = groups * slots
    depth = kernels * rows
    wide = cols + band
    hbm = pl.BlockSpec(memory_space=pltpu.HBM)
    vmem = pltpu.VMEM
    dma = pltpu.SemaphoreType.DMA
    return pl.pallas_call(
        functools.partial(body, stripes, groups, cores, half),
        out_shape=jax.ShapeDtypeStruct((rows, cols), f32),
        in_specs=[hbm] * 8,
        out_specs=pl.BlockSpec(memory_space=vmem),
        scratch_shapes=[
            *[vmem(a.shape, a.dtype) for a in (theta, seed_map, row_taps, col_taps)],
            pltpu.SMEM(weight.shape, weight.dtype),
            pltpu.SMEM((groups, slots), cond_index.dtype),
            pltpu.SMEM((groups, slots), dose.dtype),
            dma((7,)),
            vmem((rows, cols), f32),
            vmem((rows, band), bf16),
            vmem((rows, cols - band), bf16),
            vmem((span, rows, band), bf16),
            vmem((span, rows, cols - band), bf16),
            vmem((span, rows, band), bf16),
            vmem((rows, cols), bf16),
            vmem((2 * band, 2 * band), bf16),
            vmem((2 * band, cols - band), bf16),
            vmem((2 * foci * 8, 2 * band), f32),
            vmem((2 * foci * 8, 2 * band), f32),
            vmem((foci, depth, 2 * band), bf16),
            vmem((foci, span * rows, depth), bf16),
            vmem((foci * kernels, 2 * band, band), bf16),
            vmem((conds * depth, wide), bf16),
            vmem((conds * kernels, cols // band * rows, band), f32),
            vmem((conds * depth, 2 * band), bf16),
            vmem((conds * depth, cols - band), bf16),
            *[
                vmem((span, rows, width), bf16)
                for width in (band, cols - band, band, band, cols - band, band)
            ],
            dma((2, 3, span)),
            dma((2, 3, span)),
            dma,
            dma,
            *[dma((groups - 1,)) for _ in range(4)],
        ],
        compiler_params=pltpu.CompilerParams(
            collective_id=0, has_side_effects=True, vmem_limit_bytes=40 * 1024 * 1024
        ),
    )(
        *[
            pltpu.with_memory_space_constraint(a, pltpu.HBM)
            for a in (theta, seed_map, target, row_taps, col_taps, weight, cond_index, dose)
        ]
    )


def solution(mesh):
    sizes = [mesh.shape[name] for name in ("stripe", "cond", "col")]
    return jax.shard_map(
        functools.partial(shards, *sizes),
        mesh=mesh,
        in_specs=(
            P(("blocks", "stripe", "cond"), "col"),
            P(("blocks", "stripe", "cond"), "col"),
            P(("blocks", "stripe"), "col"),
            P(),
            P(),
            P(),
            P("cond"),
            P("cond"),
        ),
        out_specs=P(("blocks", "stripe", "cond"), "col"),
        check_vma=False,
    )
```

```python
import functools

import jax
import jax.numpy as jnp
from jax import lax
from jax.experimental import pallas as pl
from jax.experimental.pallas import tpu as pltpu
from jax.sharding import PartitionSpec as P

seed_shift = 1.5
steepness = 4.0
threshold = 0.3
f32 = jnp.float32
bf16 = jnp.bfloat16


def sigmoid(x):
    return 1.0 / (1.0 + jnp.exp(-x))


def toeplitz(row, count, shift):
    wide = jnp.broadcast_to(row, (count, row.shape[1]))
    return pltpu.roll(wide, shift, 1, stride=1, stride_axis=0)


def dot(a, b):
    return jnp.dot(a, b, preferred_element_type=f32)


def body(
    stripes,
    groups,
    cores,
    half,
    theta_in,
    seed_in,
    target_in,
    row_taps_in,
    col_taps_in,
    weight_in,
    cond_in,
    dose_in,
    out_ref,
    theta_ref,
    seed_ref,
    row_taps_ref,
    col_taps_ref,
    weight_ref,
    cond_ref,
    dose_ref,
    load_sem,
    sig_ref,
    own,
    edge,
    full_in,
    edge_in,
    tgt,
    ext,
    taps_pad,
    taps_rev,
    row_fwd,
    row_adj,
    col_fwd,
    row_pass,
    field,
    col_back,
    grad_full,
    grad_edge,
    part_full,
    part_edge,
    send_full,
    recv_full,
    send_edge,
    recv_edge,
    send_part,
    recv_part,
    send_rim,
    recv_rim,
    send_t,
    recv_t,
    send_c,
    recv_c,
    send_d,
    recv_d,
):
    band = 2 * half
    rows, cols = theta_ref.shape
    foci, kernels, taps = row_taps_ref.shape
    slots = cond_in.shape[0]
    reach = half // rows
    span = 2 * reach + 1
    depth = kernels * rows
    blocks = cols // band
    stripe = lax.axis_index("stripe")
    group = lax.axis_index("cond")
    core = lax.axis_index("col")
    other = cores - 1 - core
    last = stripes * groups
    mine = stripe * groups + group
    work = stripe * groups + groups - 1 - group
    side = jnp.where(group < groups // 2, -1, 1)

    def inside(at):
        return (at >= 0) & (at < last)

    def split(at):
        up = lax.div(at + groups, groups)
        return up - 1, at + groups - up * groups

    def owner(at, to_core):
        to_stripe, place = split(at)
        return {"stripe": to_stripe, "cond": place, "col": to_core}

    def worker(at, to_core):
        to_stripe, place = split(at)
        return {"stripe": to_stripe, "cond": groups - 1 - place, "col": to_core}

    def peer(group_step, to_core):
        return {"stripe": stripe, "cond": lax.rem(group + group_step, groups), "col": to_core}

    pairs = (
        (theta_in, theta_ref),
        (seed_in, seed_ref),
        (cond_in, cond_ref.at[group]),
        (dose_in, dose_ref.at[group]),
        (row_taps_in, row_taps_ref),
        (col_taps_in, col_taps_ref),
        (weight_in, weight_ref),
    )
    loads = [
        pltpu.make_async_copy(source, into, load_sem.at[i])
        for i, (source, into) in enumerate(pairs)
    ]
    barrier = pltpu.get_barrier_semaphore()

    def greet(device):
        pl.semaphore_signal(
            barrier, inc=1, device_id=device, device_id_type=pl.DeviceIdType.MESH
        )

    for j in range(1, groups):
        greet(peer(j, other))
    for d in range(-reach, reach + 1):

        @pl.when((split(work + d)[0] == stripe) & (work + d != mine))
        def _(d=d):
            greet(owner(work + d, core))

    greet(peer(0, other))
    greeted = 1 + groups - 1
    for d in range(-reach, reach + 1):
        source, target = work + d, mine + d
        source_place, target_place = split(source), split(target)
        greeted = greeted + jnp.where(
            inside(target), jnp.where(target_place[0] != stripe, cores, 0), 0
        )
        greeted = greeted + jnp.where(
            (target_place[0] == stripe) & (groups - 1 - target_place[1] != group), cores - 1, 0
        )

        @pl.when(inside(source) & (source_place[0] != stripe))
        def _(source=source):
            for c in range(cores):
                greet(owner(source, c))

    for load in loads[:2]:
        load.start()
    for load in loads[2:]:
        load.start()

    loads[0].wait()
    loads[1].wait()
    sig = sigmoid(theta_ref[...] + seed_shift * (2 * seed_ref[...] - 1).astype(f32))
    sig_ref[...] = sig
    turned = pltpu.roll(sig, half, 1).astype(bf16)
    own[...] = turned
    edge[...] = turned[:, 0:band]
    loads[2].wait()
    loads[3].wait()

    pl.semaphore_wait(barrier, greeted)

    def remote(source, target, send, recv, device):
        return pltpu.make_async_remote_copy(
            src_ref=source,
            dst_ref=target,
            send_sem=send,
            recv_sem=recv,
            device_id=device,
            device_id_type=pl.DeviceIdType.MESH,
        )

    def cond_copies(group_step):
        to = peer(group_step, other)
        at = group_step - 1
        return (
            remote(cond_ref.at[group], cond_ref.at[group], send_c.at[at], recv_c.at[at], to),
            remote(dose_ref.at[group], dose_ref.at[group], send_d.at[at], recv_d.at[at], to),
        )

    def cond_arrivals(group_step):
        source = lax.rem(group - group_step + groups, groups)
        to = peer(group_step, other)
        at = group_step - 1
        return (
            remote(cond_ref.at[source], cond_ref.at[source], send_c.at[at], recv_c.at[at], to),
            remote(dose_ref.at[source], dose_ref.at[source], send_d.at[at], recv_d.at[at], to),
        )

    def mask_full(step):
        slot = reach - step
        to = worker(mine + step, other)
        return remote(own, full_in.at[slot], send_full.at[slot], recv_full.at[slot], to)

    def mask_edge(step):
        slot = reach - step
        to = worker(mine + step, core)
        return remote(edge, edge_in.at[slot], send_edge.at[slot], recv_edge.at[slot], to)

    def full_arrival(slot):
        tile = full_in.at[slot]
        return remote(tile, tile, send_full.at[slot], recv_full.at[slot], peer(0, other))

    def edge_arrival(slot):
        tile = edge_in.at[slot]
        return remote(tile, tile, send_edge.at[slot], recv_edge.at[slot], peer(0, other))

    order = sorted(range(-reach, reach + 1), key=abs)
    def start_mask(copy, shared):
        for e in order:
            step = side * e
            at = mine + step
            wanted = inside(at)
            if not shared:
                wanted = wanted & (at != work)

            @pl.when(wanted)
            def _(step=step):
                copy(step).start()

    for group_step in range(1, groups):
        for copy in cond_copies(group_step):
            copy.start()

    start_mask(mask_edge, False)
    start_mask(mask_full, True)
    first_row = pl.multiple_of((groups - 1 - group) * rows, rows)
    target_copy = remote(
        target_in.at[pl.ds(first_row, rows), :], tgt, send_t, recv_t, peer(0, other)
    )
    target_copy.start()

    for slot in range(span):

        @pl.when(work - reach + slot == mine)
        def _(slot=slot):
            edge_in[slot] = edge[...]

        @pl.when(jnp.logical_not(inside(work - reach + slot)))
        def _(slot=slot):
            full_in[slot] = jnp.zeros((rows, cols), bf16)
            edge_in[slot] = jnp.zeros((rows, band), bf16)

        @pl.when(jnp.logical_not(inside(mine - reach + slot)))
        def _(slot=slot):
            part_full[slot] = jnp.zeros((rows, cols), bf16)
            part_edge[slot] = jnp.zeros((rows, band), bf16)

    if span * rows < 2 * band:
        ext[span * rows :, :] = jnp.zeros((2 * band - span * rows, cols + band), bf16)
    taps_pad[...] = jnp.zeros_like(taps_pad)
    mirror = (
        lax.broadcasted_iota(jnp.int32, (2 * band, 2 * band), 0)
        + lax.broadcasted_iota(jnp.int32, (2 * band, 2 * band), 1)
        == band
    ).astype(f32).astype(bf16)
    for load in loads[4:]:
        load.wait()
    for f in range(foci):
        taps_pad[f * 8 : f * 8 + kernels, 0:taps] = row_taps_ref[f].astype(f32)
        taps_pad[(foci + f) * 8 : (foci + f) * 8 + kernels, 0:taps] = col_taps_ref[f].astype(f32)
    taps_rev[...] = dot(taps_pad[...].astype(bf16), mirror)
    per = band // rows
    lane = lax.broadcasted_iota(jnp.int32, (span * rows, band), 1)
    for f in range(foci):
        for k in range(kernels):
            at = f * 8 + k
            row_fwd[f, k * rows : (k + 1) * rows, :] = toeplitz(
                taps_pad[at : at + 1, :], rows, 0
            ).astype(bf16)
        for first in range(0, kernels, per):
            tile = None
            count = min(per, kernels - first)
            for i in range(count):
                at = f * 8 + first + i
                strip = toeplitz(taps_rev[at : at + 1, :], span * rows, band + i * rows)[:, 0:band]
                tile = strip if tile is None else jnp.where(lane < i * rows, tile, strip)
            row_adj[f, :, first * rows : (first + count) * rows] = tile[:, 0 : count * rows].astype(bf16)
        for k in range(kernels):
            at = (foci + f) * 8 + k
            strip = toeplitz(taps_rev[at : at + 1, :], band, 0).astype(bf16)
            col_fwd[f * kernels + k, 0:band, :] = strip[:, band:]
            col_fwd[f * kernels + k, band:, :] = strip[:, 0:band]

    for group_step in range(1, groups):
        for copy in cond_arrivals(group_step):
            copy.wait_recv()
    for slot in range(span):
        at = work - reach + slot

        @pl.when(inside(at))
        def _(slot=slot):
            full_arrival(slot).wait_recv()

        @pl.when(inside(at) & (at != mine))
        def _(slot=slot):
            edge_arrival(slot).wait_recv()

    lanes = lax.broadcasted_iota(jnp.int32, (rows, band), 1)
    left_half = other == 0
    high = (lanes >= half).astype(f32)
    low = 1.0 - high
    high_16, low_16 = high.astype(bf16), low.astype(bf16)
    before = (low * jnp.where(left_half, 0.0, 1.0)).astype(bf16)
    after = (high * jnp.where(left_half, 1.0, 0.0)).astype(bf16)
    for slot in range(span):
        turned = full_in[slot, :, 0:band]
        rim = edge_in[slot]
        place = slice(slot * rows, (slot + 1) * rows)
        ext[place, 0:band] = turned * high_16 + rim * before
        ext[place, band:cols] = full_in[slot, :, band:]
        ext[place, cols:] = turned * low_16 + rim * after

    conds = [(g, s) for g in range(groups) for s in range(slots)]
    focus = [cond_ref[g, s] for g, s in conds]
    for c in range(len(conds)):
        row_pass[c * depth : (c + 1) * depth, :] = dot(row_fwd[focus[c]], ext[...]).astype(bf16)
    target_copy.wait_recv()
    aim = jnp.concatenate(
        [tgt[:, b * band : (b + 1) * band] for b in range(blocks)], axis=0
    ).astype(f32)
    slopes = []
    for c in range(len(conds)):
        intensity = jnp.zeros((blocks * rows, band), f32)
        for k in range(kernels):
            first = c * depth + k * rows
            left = jnp.concatenate(
                [
                    row_pass[first : first + rows, b * band : (b + 2) * band]
                    for b in range(blocks)
                ],
                axis=0,
            )
            amp = dot(left, col_fwd[focus[c] * kernels + k])
            field[c * kernels + k] = amp
            intensity = intensity + weight_ref[focus[c], k] * (amp * amp)
        slopes.append(intensity)
    for c, (g, s) in enumerate(conds):
        dose = dose_ref[g, s]
        resist = sigmoid(steepness * (dose * slopes[c] - threshold))
        slopes[c] = (2.0 * steepness) * (resist - aim) * dose * resist * (1.0 - resist)
    for c in range(len(conds)):
        for k in range(kernels):
            weight = 2.0 * weight_ref[focus[c], k]
            dfield = (weight * field[c * kernels + k] * slopes[c]).astype(bf16)
            spread = lax.dot_general(
                dfield,
                col_fwd[focus[c] * kernels + k],
                (((1,), (1,)), ((), ())),
                preferred_element_type=f32,
            )
            first = c * depth + k * rows
            for b in range(blocks + 1):
                piece = None
                if b < blocks:
                    piece = spread[b * rows : (b + 1) * rows, 0:band]
                if b > 0:
                    more = spread[(b - 1) * rows : b * rows, band:]
                    piece = more if piece is None else piece + more
                col_back[first : first + rows, b * band : (b + 1) * band] = piece.astype(bf16)

    if depth % band == 0:
        total = dot(
            jnp.concatenate([row_adj[focus[c]] for c in range(len(conds))], axis=1), col_back[...]
        )
    else:
        total = jnp.zeros((span * rows, cols + band), f32)
        for c in range(len(conds)):
            total = total + dot(row_adj[focus[c]], col_back[c * depth : (c + 1) * depth, :])

    for slot in range(span):
        rows_of = total[slot * rows : (slot + 1) * rows, :]
        head, tail = rows_of[:, 0:band], rows_of[:, cols:]
        grad_full[slot, :, 0:band] = jnp.where(lanes >= half, head, tail).astype(bf16)
        grad_full[slot, :, band:] = rows_of[:, band:cols].astype(bf16)
        grad_edge[slot] = jnp.where(left_half, tail * high, head * low).astype(bf16)

    def part_copy(slot):
        into = 2 * reach - slot
        to = owner(work - reach + slot, other)
        return remote(
            grad_full.at[slot], part_full.at[into], send_part.at[into], recv_part.at[into], to
        )

    def rim_copy(slot):
        into = 2 * reach - slot
        to = owner(work - reach + slot, core)
        return remote(
            grad_edge.at[slot], part_edge.at[into], send_rim.at[into], recv_rim.at[into], to
        )

    def part_arrival(slot):
        tile = part_full.at[slot]
        return remote(tile, tile, send_part.at[slot], recv_part.at[slot], peer(0, other))

    def rim_arrival(slot):
        tile = part_edge.at[slot]
        return remote(tile, tile, send_rim.at[slot], recv_rim.at[slot], peer(0, other))

    for e in order:
        slot = reach - side * e
        at = work - reach + slot

        @pl.when(inside(at) & (at != mine))
        def _(slot=slot):
            rim_copy(slot).start()

    for e in order:
        slot = reach - side * e

        @pl.when(inside(work - reach + slot))
        def _(slot=slot):
            part_copy(slot).start()

    for slot in range(span):

        @pl.when(work - reach + slot == mine)
        def _(slot=slot):
            part_edge[2 * reach - slot] = grad_edge[slot]

    for slot in range(span):
        at = mine - reach + slot

        @pl.when(inside(at))
        def _(slot=slot):
            part_arrival(slot).wait_recv()

        @pl.when(inside(at) & (at != work))
        def _(slot=slot):
            rim_arrival(slot).wait_recv()

    sums = jnp.zeros((rows, cols), f32)
    rims = jnp.zeros((rows, band), f32)
    for slot in range(span):
        sums = sums + part_full[slot].astype(f32)
        rims = rims + part_edge[slot].astype(f32)
    sums = jnp.concatenate([sums[:, 0:band] + rims, sums[:, band:]], axis=1)
    sig = sig_ref[...]
    out_ref[...] = pltpu.roll(sums, cols - half, 1) * sig * (1.0 - sig)

    for group_step in range(1, groups):
        for copy in cond_copies(group_step):
            copy.wait_send()
    target_copy.wait_send()
    for e in order:
        step = side * e
        slot = reach - side * e
        at = work - reach + slot

        @pl.when(inside(mine + step))
        def _(step=step):
            mask_full(step).wait_send()

        @pl.when(inside(mine + step) & (mine + step != work))
        def _(step=step):
            mask_edge(step).wait_send()

        @pl.when(inside(at))
        def _(slot=slot):
            part_copy(slot).wait_send()

        @pl.when(inside(at) & (at != mine))
        def _(slot=slot):
            rim_copy(slot).wait_send()


def shards(stripes, groups, cores, theta, seed_map, target, row_taps, col_taps, weight, cond_index, dose):
    rows, cols = theta.shape
    foci, kernels, taps = row_taps.shape
    half = taps // 2
    band = 2 * half
    span = 2 * (half // rows) + 1
    slots = cond_index.shape[0]
    conds = groups * slots
    depth = kernels * rows
    wide = cols + band
    hbm = pl.BlockSpec(memory_space=pltpu.HBM)
    vmem = pltpu.VMEM
    dma = pltpu.SemaphoreType.DMA
    return pl.pallas_call(
        functools.partial(body, stripes, groups, cores, half),
        out_shape=jax.ShapeDtypeStruct((rows, cols), f32),
        in_specs=[hbm] * 8,
        out_specs=pl.BlockSpec(memory_space=vmem),
        scratch_shapes=[
            *[vmem(a.shape, a.dtype) for a in (theta, seed_map, row_taps, col_taps)],
            pltpu.SMEM(weight.shape, weight.dtype),
            pltpu.SMEM((groups, slots), cond_index.dtype),
            pltpu.SMEM((groups, slots), dose.dtype),
            dma((7,)),
            vmem((rows, cols), f32),
            vmem((rows, cols), bf16),
            vmem((rows, band), bf16),
            vmem((span, rows, cols), bf16),
            vmem((span, rows, band), bf16),
            vmem((rows, cols), bf16),
            vmem((2 * band, wide), bf16),
            vmem((2 * foci * 8, 2 * band), f32),
            vmem((2 * foci * 8, 2 * band), f32),
            vmem((foci, depth, 2 * band), bf16),
            vmem((foci, span * rows, depth), bf16),
            vmem((foci * kernels, 2 * band, band), bf16),
            vmem((conds * depth, wide), bf16),
            vmem((conds * kernels, cols // band * rows, band), f32),
            vmem((conds * depth, wide), bf16),
            vmem((span, rows, cols), bf16),
            vmem((span, rows, band), bf16),
            vmem((span, rows, cols), bf16),
            vmem((span, rows, band), bf16),
            *[dma((span,)) for _ in range(8)],
            dma,
            dma,
            *[dma((groups - 1,)) for _ in range(4)],
        ],
        compiler_params=pltpu.CompilerParams(
            collective_id=0, has_side_effects=True, vmem_limit_bytes=40 * 1024 * 1024
        ),
    )(
        *[
            pltpu.with_memory_space_constraint(a, pltpu.HBM)
            for a in (theta, seed_map, target, row_taps, col_taps, weight, cond_index, dose)
        ]
    )


def solution(mesh):
    sizes = [mesh.shape[name] for name in ("stripe", "cond", "col")]
    return jax.shard_map(
        functools.partial(shards, *sizes),
        mesh=mesh,
        in_specs=(
            P(("blocks", "stripe", "cond"), "col"),
            P(("blocks", "stripe", "cond"), "col"),
            P(("blocks", "stripe"), "col"),
            P(),
            P(),
            P(),
            P("cond"),
            P("cond"),
        ),
        out_specs=P(("blocks", "stripe", "cond"), "col"),
        check_vma=False,
    )
```
